32 devices in a mesh: head: 4 (over z), seq: 8 (over y, x, core).
Axes of the slice: x: 2, y: 2, z: 4, core: 2. Of those that a mesh axis runs over, the one named last changes fastest.
Arguments:
- keys: bfloat16 [2, 4096, 2560], P(None, 'seq', 'head'), may hold values from -6 to 6
- values: bfloat16 [2, 4096, 2560], P(None, 'seq', 'head'), may hold values from -6 to 6
- step_rates: float32 [2, 4, 4096], P(None, 'head', 'seq'), may hold values from 0.05 to 1
- queries: bfloat16 [4096, 2560], P('seq', 'head'), may hold values from -6 to 6
- first_weight: bfloat16 [4, 640, 640], P('head'), may hold values from -0.25 to 0.25
- third_weight: bfloat16 [4, 640, 640], P('head'), may hold values from -0.25 to 0.25
- second_weight: bfloat16 [4, 640, 640], P('head'), may hold values from -0.25 to 0.25
- out_weight: bfloat16 [2560, 2560], P('head'), may hold values from -0.125 to 0.125
- live_counts: int32 [3, 8], P(None, 'seq'), may hold values from 256 to 512
Outputs:
- mixed: bfloat16 [4096, 2560], P('seq', 'head')
The draws below stay inside these ranges and needn't reach their ends.
Inputs may be any that keep to these rules, and one draw needn't show every extreme that they name: `live_counts`: the live rows of a shard are its first ones.
All inputs are finite; a program needn't handle non-finite values.
Results may differ from the reference program's by a relative error of at most 0.023.
Values may be sent and summed in bfloat16 or wider, within the bound.
A program may use at most 128 MiB of HBM per device.

```python
import math
import jax
import jax.numpy as jnp
from jax import lax

DH = 640
FH = 640
TOK_DEV = 512
GROUPS = 2
NS_ITERS = 3
HEADS = 4
D = 2560
TOKENS = 4096
SHARDS = 8


def set_ends(values, rng, low, largest):
    index_at = [jax.random.randint(jax.random.fold_in(rng, axis), (), 0, length) for axis, length in enumerate(values.shape)]
    widest = values.shape.index(max(values.shape))
    neighbour = index_at[:widest] + [(index_at[widest] + 1) % values.shape[widest]] + index_at[widest + 1:]
    return values.at[tuple(index_at)].set(low).at[tuple(neighbour)].set(largest)


def block_scale(rng, shape, split, low, high):
    level = 1.0
    for position, blocks in split:
        steps = jax.random.uniform(jax.random.fold_in(jax.random.fold_in(rng, 6), position), (blocks,), jnp.float32, low / len(split), high / len(split))
        level = level * jnp.repeat(jnp.exp(steps), shape[position] // blocks).reshape((-1,) + (1,) * (len(shape) - 1 - position))
    return level


def gaussian(stream_key, extent, scale, most, split=(), held_as=jnp.bfloat16):
    values = scale * jax.random.normal(stream_key, extent, jnp.float32)
    if split:
        values = values * block_scale(stream_key, extent, split, -0.22, 0.18)
    return jnp.clip(values, -most, most).astype(held_as)


def setup_inputs(seed: int = 0) -> dict:
    arg_keys = jax.random.split(jax.random.key(seed), 10)
    return {
        "keys": gaussian(arg_keys[0], (GROUPS, TOKENS, D), 1.0, 6.0, ((1, 8), (2, 4))),
        "values": gaussian(arg_keys[1], (GROUPS, TOKENS, D), 1.0, 6.0, ((1, 8), (2, 4))),
        "step_rates": jnp.clip(jnp.exp(math.log(1.0) - 2.9957323 * jax.random.uniform(arg_keys[2], (GROUPS, HEADS, TOKENS), jnp.float32) ** block_scale(arg_keys[2], (GROUPS, HEADS, TOKENS), ((1, 4), (2, 8)), -0.2, 0.2)), 0.05, 1.0),
        "queries": gaussian(arg_keys[3], (TOKENS, D), 1.0, 6.0, ((0, 8), (1, 4))),
        "first_weight": gaussian(arg_keys[4], (HEADS, DH, FH), DH ** -0.5, 0.25, ((0, 4),)),
        "third_weight": gaussian(arg_keys[5], (HEADS, DH, FH), DH ** -0.5, 0.25, ((0, 4),)),
        "second_weight": gaussian(arg_keys[6], (HEADS, FH, DH), FH ** -0.5, 0.25, ((0, 4),)),
        "out_weight": gaussian(arg_keys[7], (D, D), D ** -0.5, 0.125, ((0, 4),)),
        "live_counts": set_ends(jax.random.randint(arg_keys[8], (GROUPS + 1, SHARDS), TOK_DEV // 2, TOK_DEV + 1), jax.random.fold_in(arg_keys[8], 1), TOK_DEV // 2, TOK_DEV).astype(jnp.int32),
    }


coef_a = 3.4445
coef_b = -4.775
coef_c = 2.0315
step_size = 0.5

def fast_grads(inputs, targets, scaling, first, third, second):
    first_pre = jnp.dot(inputs, first, preferred_element_type=jnp.float32)
    third_pre = jnp.dot(inputs, third, preferred_element_type=jnp.float32)
    sigmoid = jax.nn.sigmoid(first_pre)
    swish = first_pre * sigmoid
    hidden = (swish * third_pre).astype(jnp.bfloat16)
    weighted = (targets.astype(jnp.float32) * scaling[:, None]).astype(jnp.bfloat16)
    grad_second = jnp.dot(hidden.T, weighted, preferred_element_type=jnp.float32)
    back = jnp.dot(weighted, second.T, preferred_element_type=jnp.float32)
    back_first = (back * third_pre * sigmoid * (1.0 + first_pre * (1.0 - sigmoid))).astype(jnp.bfloat16)
    back_third = (back * swish).astype(jnp.bfloat16)
    grad_first = jnp.dot(inputs.T, back_first, preferred_element_type=jnp.float32)
    grad_third = jnp.dot(inputs.T, back_third, preferred_element_type=jnp.float32)
    return (grad_first, grad_third, grad_second)

def orthogonal(gradient):
    scale = jnp.sqrt(jnp.sum(gradient * gradient)) + 1e-06
    current = (gradient / scale).astype(jnp.bfloat16)
    for index in range(NS_ITERS):
        gram_wide = jnp.dot(current, current.T, preferred_element_type=jnp.float32)
        gram_low = gram_wide.astype(jnp.bfloat16)
        poly = (coef_b * gram_wide + coef_c * jnp.dot(gram_low, gram_low, preferred_element_type=jnp.float32)).astype(jnp.bfloat16)
        current = (coef_a * current.astype(jnp.float32) + jnp.dot(poly, current, preferred_element_type=jnp.float32)).astype(jnp.bfloat16)
    return current

def renewed(weight, gradient):
    old = weight.astype(jnp.float32)
    fresh = old + step_size * orthogonal(gradient).astype(jnp.float32)
    ratio = jnp.sqrt(lax.optimization_barrier(jnp.mean(old * old, axis=0)) + 1e-06) / jnp.sqrt(lax.optimization_barrier(jnp.mean(fresh * fresh, axis=0)) + 1e-06)
    return (fresh * ratio[None, :]).astype(jnp.bfloat16)

def applied(inputs, first, third, second, live):
    first_pre = jnp.dot(inputs, first, preferred_element_type=jnp.float32)
    third_pre = jnp.dot(inputs, third, preferred_element_type=jnp.float32)
    hidden = (jax.nn.silu(first_pre) * third_pre).astype(jnp.bfloat16)
    result = jnp.dot(hidden, second, preferred_element_type=jnp.float32)
    return (result * live[:, None]).astype(jnp.bfloat16)

def reference(keys, values, step_rates, queries, first_weight, third_weight, second_weight, out_weight, live_counts):
    indices = jnp.arange(TOKENS).astype(jnp.int32)
    positions = indices % TOK_DEV
    owners = indices // TOK_DEV
    outputs = []
    for head in range(HEADS):
        lower = head * DH
        totals = None
        for group in range(GROUPS):
            live = (positions < live_counts[group][owners]).astype(jnp.float32)
            scaling = live * step_rates[group, head]
            parts = fast_grads(keys[group][:, lower:lower + DH], values[group][:, lower:lower + DH], scaling, first_weight[head], third_weight[head], second_weight[head])
            totals = parts if totals is None else tuple((a + b for a, b in zip(totals, parts)))
        new_first = renewed(first_weight[head], totals[0])
        new_third = renewed(third_weight[head], totals[1])
        new_second = renewed(second_weight[head], totals[2])
        live_query = (positions < live_counts[GROUPS][owners]).astype(jnp.float32)
        outputs.append(applied(queries[:, lower:lower + DH], new_first, new_third, new_second, live_query))
    merged = jnp.concatenate(outputs, axis=1)
    return jnp.dot(merged, out_weight, preferred_element_type=jnp.float32).astype(jnp.bfloat16)
```

```python
import functools

import jax
import jax.numpy as jnp
from jax import lax
from jax.experimental import pallas as pl
from jax.experimental.pallas import tpu as pltpu
from jax.sharding import PartitionSpec as P

NS_ITERS = 3
coef_a = 3.4445
coef_b = -4.775
coef_c = 2.0315
step_size = 0.5

MESH = pl.DeviceIdType.MESH
F32 = jnp.float32
BF16 = jnp.bfloat16


def dot(left, right, dims=((1,), (0,))):
    return lax.dot_general(left, right, (dims, ((), ())), preferred_element_type=F32)


def kernel(
    heads, shards, tile,
    keys, values, scaling, queries, live_query, first, third, second, out_weight,
    mixed,
    gate_s, swish_s, hidden_s, weighted_s, back_first_s, back_third_s,
    wide, gram_s, current, poly_s, fresh_w,
    send_a, recv_a, send_b, recv_b, full, columns, head_out,
    ag_right, ag_left, rs_right, rs_left, rs_send_right, rs_send_left, total_ag,
    sem_a, sem_b, sem_c, sem_d, sem_w, sem_x, sem_ag, sem_rs,
):
    chips = shards // 2
    rows, width = keys.shape
    grad_rows = width // shards
    z = lax.axis_index("head")
    s = lax.axis_index("seq")
    core = lax.rem(s, 2)
    chip = s // 2
    partner = {"seq": s + 1 - 2 * core}
    half = width // 2
    tokens = queries.shape[0]
    part = tokens // 2

    def peer(distance):
        return {"seq": 2 * lax.rem(chip + distance, chips) + core}

    def z_peer(distance):
        return {"head": lax.rem(z + distance, heads)}

    def remote(source, target, sems, device):
        return pltpu.make_async_remote_copy(
            src_ref=source, dst_ref=target, send_sem=sems[0], recv_sem=sems[1],
            device_id=device, device_id_type=MESH,
        )

    barrier = pltpu.get_barrier_semaphore()
    greeted = [partner] + [peer(k) for k in range(1, chips)] + [z_peer(k) for k in range(1, heads)]
    for device in greeted:
        pl.semaphore_signal(barrier, inc=1, device_id=device, device_id_type=MESH)
    pl.semaphore_wait(barrier, len(greeted))

    core_rows = pl.ds(pl.multiple_of(core * half, 16), half)

    def weight_copy(k):
        dest = lax.rem(z + k, heads)
        return remote(
            out_weight.at[core_rows, pl.ds(pl.multiple_of(dest * width, 128), width)],
            columns.at[z, core_rows],
            (sem_w.at[0, k], sem_w.at[1, k]),
            z_peer(k),
        )

    def weight_share(k):
        block = columns.at[lax.rem(z + heads - k, heads), core_rows]
        return remote(block, block, (sem_x.at[0, k], sem_x.at[1, k]), partner)

    for k in sorted(range(1, heads), key=lambda k: -abs(k - heads / 2)):
        weight_copy(k).start()

    def copy_a(m):
        return remote(send_a.at[m, 1 - core], recv_a.at[m], (sem_a.at[0, m], sem_a.at[1, m]), partner)

    def copy_b(m, k):
        return remote(
            send_b.at[m, lax.rem(chip + k, chips)], recv_b.at[m, k - 1],
            (sem_b.at[0, m, k], sem_b.at[1, m, k]), peer(k),
        )

    def copy_c(m, k):
        block = full.at[m, core, chip]
        return remote(block, block, (sem_c.at[0, m, k], sem_c.at[1, m, k]), peer(k))

    def copy_d(m):
        return remote(full.at[m, core], full.at[m, core], (sem_d.at[0, m], sem_d.at[1, m]), partner)

    def start_a(m):
        for index in range(shards):
            send_a[m, index % 2, index // 2] = wide[index * grad_rows:(index + 1) * grad_rows, :].astype(BF16)
        copy_a(m).start()

    def step_b(m):
        copy_a(m).wait_recv()
        send_b[m] = (send_a[m, core].astype(F32) + recv_a[m].astype(F32)).astype(BF16)
        for k in range(1, chips):
            copy_b(m, k).start()

    def step_c(m):
        for k in range(1, chips):
            copy_b(m, k).wait_recv()
        total = send_b[m, chip].astype(F32)
        for k in range(1, chips):
            total = total + recv_b[m, k - 1].astype(F32)
        full[m, core, chip] = total.astype(BF16)
        for k in range(1, chips):
            copy_c(m, k).start()

    def step_d(m):
        for k in range(1, chips):
            copy_c(m, k).wait_recv()
        copy_d(m).start()

    def step_e(m):
        copy_d(m).wait_recv()

    @pl.loop(0, rows // tile)
    def _(index):
        at = pl.ds(pl.multiple_of(index * tile, tile), tile)
        k = keys[at, :]
        first_pre = dot(k, first[...])
        third_pre = dot(k, third[...])
        sig = jax.nn.sigmoid(first_pre)
        swish = first_pre * sig
        hidden_s[at, :] = (swish * third_pre).astype(BF16)
        swish_s[at, :] = swish
        gate_s[at, :] = third_pre * sig * (1.0 + first_pre * (1.0 - sig))
        weighted_s[at, :] = (values[at, :].astype(F32) * scaling[at, :]).astype(BF16)

    wide[...] = dot(hidden_s[...], weighted_s[...], ((0,), (0,)))
    start_a(0)

    @pl.loop(0, rows // tile)
    def _(index):
        at = pl.ds(pl.multiple_of(index * tile, tile), tile)
        back = dot(weighted_s[at, :], second[...], ((1,), (1,)))
        back_third_s[at, :] = (back * swish_s[at, :]).astype(BF16)
        back_first_s[at, :] = (back * gate_s[at, :]).astype(BF16)

    wide[...] = dot(keys[...], back_third_s[...], ((0,), (0,)))
    start_a(1)
    step_b(0)
    wide[...] = dot(keys[...], back_first_s[...], ((0,), (0,)))
    start_a(2)
    step_b(1)
    step_c(0)
    step_b(2)
    step_c(1)
    step_d(0)
    step_e(0)

    def renew(weight, slot):
        old = weight[...].astype(F32)
        fresh = old + step_size * current[...].astype(F32)
        ratio = jnp.sqrt(jnp.mean(old * old, axis=0, keepdims=True) + 1e-06) / jnp.sqrt(
            jnp.mean(fresh * fresh, axis=0, keepdims=True) + 1e-06
        )
        fresh_w[slot] = (fresh * ratio).astype(BF16)

    @pl.loop(0, 3 * NS_ITERS)
    def _(t):
        @pl.when(t == 1)
        def _():
            step_c(2)

        @pl.when(t == 2)
        def _():
            step_d(1)

        @pl.when(t == NS_ITERS)
        def _():
            step_e(1)

        @pl.when(t == NS_ITERS + 1)
        def _():
            step_d(2)

        @pl.when(t == 2 * NS_ITERS)
        def _():
            step_e(2)

        @pl.when(t == 2 * NS_ITERS + 1)
        def _():
            for k in range(1, heads):
                weight_copy(k).wait_recv()
                weight_share(k).start()

        @pl.when(lax.rem(t, NS_ITERS) == 0)
        def _():
            m = t // NS_ITERS
            for index in range(shards):
                wide[index * grad_rows:(index + 1) * grad_rows, :] = full[m, index % 2, index // 2].astype(F32)
            gradient = wide[...]
            square = jnp.sum(jnp.sum(gradient * gradient, axis=0, keepdims=True), axis=1, keepdims=True)
            current[...] = (gradient / (jnp.sqrt(square) + 1e-06)).astype(BF16)

        gram_wide = dot(current[...], current[...], ((1,), (1,)))
        wide[...] = gram_wide
        gram_s[...] = gram_wide.astype(BF16)
        poly_s[...] = (coef_b * wide[...] + coef_c * dot(gram_s[...], gram_s[...])).astype(BF16)
        current[...] = (coef_a * current[...].astype(F32) + dot(poly_s[...], current[...])).astype(BF16)

        @pl.when(t == NS_ITERS - 1)
        def _():
            renew(second, 2)

        @pl.when(t == 2 * NS_ITERS - 1)
        def _():
            renew(third, 1)

        @pl.when(t == 3 * NS_ITERS - 1)
        def _():
            renew(first, 0)

    @pl.loop(0, tokens // tile)
    def _(index):
        at = pl.ds(pl.multiple_of(index * tile, tile), tile)
        q = queries[at, :]
        first_pre = dot(q, fresh_w[0])
        third_pre = dot(q, fresh_w[1])
        hidden = (first_pre * jax.nn.sigmoid(first_pre) * third_pre).astype(BF16)
        head_out[at, :] = (dot(hidden, fresh_w[2]) * live_query[at, :]).astype(BF16)

    gather_half = head_out.at[pl.ds(0, part)]
    last = heads - 1
    sides = {
        "right": (z, z + 1, ag_right, rs_right, rs_send_right, 0),
        "left": (last - z, z - 1, ag_left, rs_left, rs_send_left, 1),
    }

    def ag_copy(side, k):
        place, neighbour, slots, _, _, d = sides[side]
        source = gather_half if k == 1 else slots.at[k - 2]
        return remote(source, slots.at[k - 1], (sem_ag.at[0, d, k], sem_ag.at[1, d, k]), {"head": neighbour})

    def rs_copy(side, k):
        place, neighbour, _, slots, sends, d = sides[side]
        return remote(sends.at[k - 1], slots.at[k - 1], (sem_rs.at[0, d, k], sem_rs.at[1, d, k]), {"head": neighbour})

    def projected(dest):
        cols = pl.ds(pl.multiple_of(dest * width, 128), width)
        return dot(head_out[part:, :], out_weight[:, cols])

    def round_sends(side, k):
        place, _, _, slots, sends, _ = sides[side]

        @pl.when((place <= k - 1) & (place < last))
        def _():
            dest = heads - k + z if side == "right" else k + z - heads
            mine = projected(dest)
            if k == 1:
                sends[0] = mine.astype(BF16)
            else:
                @pl.when(place == 0)
                def _():
                    sends[k - 1] = mine.astype(BF16)

                @pl.when(place >= 1)
                def _():
                    rs_copy(side, k - 1).wait_recv()
                    sends[k - 1] = (mine + slots[k - 2].astype(F32)).astype(BF16)

            rs_copy(side, k).start()

        @pl.when(place >= k - 1)
        def _():
            if k > 1:
                ag_copy(side, k - 1).wait_recv()

            @pl.when(place < last)
            def _():
                ag_copy(side, k).start()

    def gathered(side, k):
        place, _, slots, _, _, _ = sides[side]

        @pl.when(place >= k)
        def _():
            origin = z - k if side == "right" else z + k
            total_ag[...] += dot(slots[k - 1], columns[origin])

    for k in range(1, heads):
        @pl.when(2 * z < heads)
        def _():
            round_sends("left", k)
            round_sends("right", k)

        @pl.when(2 * z >= heads)
        def _():
            round_sends("right", k)
            round_sends("left", k)

        if k == 1:
            own = pl.ds(pl.multiple_of(z * width, 128), width)
            total_ag[...] = dot(head_out[:part, :], out_weight[:, own])
            wide[:part, :] = projected(z)
            for j in range(1, heads):
                weight_share(j).wait_recv()
        else:
            gathered("left", k - 1)
            gathered("right", k - 1)

    for side in ("left", "right"):
        place, _, ag_slots, rs_slots, _, _ = sides[side]

        @pl.when(place >= last)
        def _():
            ag_copy(side, last).wait_recv()

        gathered(side, last)

        @pl.when(place >= 1)
        def _():
            rs_copy(side, last).wait_recv()
            wide[:part, :] += rs_slots[last - 1].astype(F32)

    mixed[:part, :] = total_ag[...].astype(BF16)
    mixed[part:, :] = wide[:part, :].astype(BF16)

    for m in range(3):
        copy_a(m).wait_send()
        copy_d(m).wait_send()
        for k in range(1, chips):
            copy_b(m, k).wait_send()
            copy_c(m, k).wait_send()
    for k in range(1, heads):
        weight_copy(k).wait_send()
        weight_share(k).wait_send()
        for side in ("left", "right"):
            place = sides[side][0]

            @pl.when((place <= k - 1) & (place < last))
            def _():
                rs_copy(side, k).wait_send()

            @pl.when((place >= k - 1) & (place < last))
            def _():
                ag_copy(side, k).wait_send()


def on_device(
    heads, shards,
    keys, values, step_rates, queries, first_weight, third_weight, second_weight, out_weight, live_counts,
):
    groups, rows, width = keys.shape
    chips = shards // 2
    grad_rows = width // shards
    part = rows // 2
    positions = jnp.arange(rows, dtype=jnp.int32)
    live = (positions[None, :] < live_counts).astype(F32)
    scaling = (live[:groups] * step_rates[:, 0]).reshape(groups * rows, 1)
    live_query = live[groups].reshape(rows, 1)
    every = groups * rows
    vmem = pl.BlockSpec(memory_space=pltpu.VMEM)
    dma = pltpu.SemaphoreType.DMA
    return pl.pallas_call(
        functools.partial(kernel, heads, shards, 256),
        out_shape=jax.ShapeDtypeStruct((rows, width), BF16),
        in_specs=[vmem] * 9,
        out_specs=vmem,
        scratch_shapes=[
            pltpu.VMEM((every, width), F32),
            pltpu.VMEM((every, width), F32),
            pltpu.VMEM((every, width), BF16),
            pltpu.VMEM((every, width), BF16),
            pltpu.VMEM((every, width), BF16),
            pltpu.VMEM((every, width), BF16),
            pltpu.VMEM((width, width), F32),
            pltpu.VMEM((width, width), BF16),
            pltpu.VMEM((width, width), BF16),
            pltpu.VMEM((width, width), BF16),
            pltpu.VMEM((3, width, width), BF16),
            pltpu.VMEM((3, 2, chips, grad_rows, width), BF16),
            pltpu.VMEM((3, chips, grad_rows, width), BF16),
            pltpu.VMEM((3, chips, grad_rows, width), BF16),
            pltpu.VMEM((3, chips - 1, grad_rows, width), BF16),
            pltpu.VMEM((3, 2, chips, grad_rows, width), BF16),
            pltpu.VMEM((heads, width, width), BF16),
            pltpu.VMEM((rows, width), BF16),
        ]
        + [pltpu.VMEM((heads - 1, part, width), BF16)] * 6
        + [
            pltpu.VMEM((part, width), F32),
            dma((2, 3)),
            dma((2, 3, chips)),
            dma((2, 3, chips)),
            dma((2, 3)),
            dma((2, heads)),
            dma((2, heads)),
            dma((2, 2, heads)),
            dma((2, 2, heads)),
        ],
        compiler_params=pltpu.CompilerParams(
            collective_id=0, has_side_effects=True, vmem_limit_bytes=67000000
        ),
        name="fast_weight_layer",
    )(
        keys.reshape(every, width), values.reshape(every, width), scaling, queries, live_query,
        first_weight[0], third_weight[0], second_weight[0], out_weight,
    )


def solution(mesh):
    in_specs = (
        P(None, "seq", "head"),
        P(None, "seq", "head"),
        P(None, "head", "seq"),
        P("seq", "head"),
        P("head", None, None),
        P("head", None, None),
        P("head", None, None),
        P("head", None),
        P(None, "seq"),
    )
    return jax.shard_map(
        functools.partial(on_device, mesh.shape["head"], mesh.shape["seq"]),
        mesh=mesh, in_specs=in_specs, out_specs=P("seq", "head"), check_vma=False,
    )
```

```python
import functools

import jax
import jax.numpy as jnp
from jax import lax
from jax.experimental import pallas as pl
from jax.experimental.pallas import tpu as pltpu
from jax.sharding import PartitionSpec as P

NS_ITERS = 3
coef_a = 3.4445
coef_b = -4.775
coef_c = 2.0315
step_size = 0.5

MESH = pl.DeviceIdType.MESH
F32 = jnp.float32
BF16 = jnp.bfloat16


def dot(left, right, dims=((1,), (0,))):
    return lax.dot_general(left, right, (dims, ((), ())), preferred_element_type=F32)


def kernel(
    heads, shards, tile,
    keys_in, values_in, rates, queries_in, first_in, third_in, second_in, weight_in, counts,
    mixed,
    keys, values, queries, first, third, second, out_weight, scaling,
    gate_s, swish_s, hidden_s, weighted_s, back_first_s, back_third_s,
    wide, gram_s, current, poly_s, fresh_w,
    send_a, recv_a, send_b, recv_b, full, columns, head_out,
    ag_right, ag_left, rs_right, rs_left, rs_send_right, rs_send_left, total_ag,
    sem_a, sem_b, sem_c, sem_d, sem_w, sem_x, sem_ag, sem_rs,
    sem_in, sem_tile,
):
    chips = shards // 2
    rows, width = keys.shape
    groups, group_rows = rates.shape
    grad_rows = width // shards
    z = lax.axis_index("head")
    s = lax.axis_index("seq")
    core = lax.rem(s, 2)
    chip = s // 2
    partner = {"seq": s + 1 - 2 * core}
    half = width // 2
    tokens = queries.shape[0]
    part = tokens // 2

    def peer(distance):
        return {"seq": 2 * lax.rem(chip + distance, chips) + core}

    def z_peer(distance):
        return {"head": lax.rem(z + distance, heads)}

    def remote(source, target, sems, device):
        return pltpu.make_async_remote_copy(
            src_ref=source, dst_ref=target, send_sem=sems[0], recv_sem=sems[1],
            device_id=device, device_id_type=MESH,
        )

    def tile_copy(index, which):
        at = pl.ds(pl.multiple_of(index * tile, tile), tile)
        source, target = ((keys_in, keys), (values_in, values))[which]
        return pltpu.make_async_copy(source.at[at], target.at[at], sem_tile.at[which, index])

    def input_copy(index):
        source, target = (
            (first_in, first), (third_in, third), (second_in, second), (queries_in, queries), (weight_in, out_weight),
        )[index]
        return pltpu.make_async_copy(source, target, sem_in.at[index])

    input_copy(0).start()
    input_copy(1).start()
    for index in range(rows // tile):
        tile_copy(index, 0).start()
        tile_copy(index, 1).start()
    for index in range(2, 5):
        input_copy(index).start()

    barrier = pltpu.get_barrier_semaphore()
    greeted = [partner] + [peer(k) for k in range(1, chips)] + [z_peer(k) for k in range(1, heads)]
    for device in greeted:
        pl.semaphore_signal(barrier, inc=1, device_id=device, device_id_type=MESH)
    pl.semaphore_wait(barrier, len(greeted))

    core_rows = pl.ds(pl.multiple_of(core * half, 16), half)

    def weight_copy(k):
        dest = lax.rem(z + k, heads)
        return remote(
            weight_in.at[core_rows, pl.ds(pl.multiple_of(dest * width, 128), width)],
            columns.at[z, core_rows],
            (sem_w.at[0, k], sem_w.at[1, k]),
            z_peer(k),
        )

    def weight_share(k):
        block = columns.at[lax.rem(z + heads - k, heads), core_rows]
        return remote(block, block, (sem_x.at[0, k], sem_x.at[1, k]), partner)

    for k in sorted(range(1, heads), key=lambda k: -abs(k - heads / 2)):
        weight_copy(k).start()

    def copy_a(m):
        return remote(send_a.at[m, 1 - core], recv_a.at[m], (sem_a.at[0, m], sem_a.at[1, m]), partner)

    cut = (grad_rows // 2 + 15) // 16 * 16
    pieces = (pl.ds(0, cut), pl.ds(cut, grad_rows - cut))

    def copy_b(m, k, p):
        return remote(
            send_b.at[m, lax.rem(chip + k, chips), pieces[p]], recv_b.at[m, k - 1, pieces[p]],
            (sem_b.at[0, m, k, p], sem_b.at[1, m, k, p]), peer(k),
        )

    def copy_c(m, k, p):
        block = full.at[m, core, chip, pieces[p]]
        return remote(block, block, (sem_c.at[0, m, k, p], sem_c.at[1, m, k, p]), peer(k))

    def copy_d(m, p):
        block = full.at[m, core, :, pieces[p]]
        return remote(block, block, (sem_d.at[0, m, p], sem_d.at[1, m, p]), partner)

    def start_a(m):
        for index in range(shards):
            send_a[m, index % 2, index // 2] = wide[index * grad_rows:(index + 1) * grad_rows, :].astype(BF16)
        copy_a(m).start()

    def step_b(m):
        copy_a(m).wait_recv()
        send_b[m] = (send_a[m, core].astype(F32) + recv_a[m].astype(F32)).astype(BF16)
        for p in range(2):
            for k in range(1, chips):
                copy_b(m, k, p).start()

    def step_c(m):
        for p in range(2):
            for k in range(1, chips):
                copy_b(m, k, p).wait_recv()
            total = send_b[m, chip, pieces[p]].astype(F32)
            for k in range(1, chips):
                total = total + recv_b[m, k - 1, pieces[p]].astype(F32)
            full[m, core, chip, pieces[p]] = total.astype(BF16)
            for k in range(1, chips):
                copy_c(m, k, p).start()

    def step_d(m):
        for p in range(2):
            for k in range(1, chips):
                copy_c(m, k, p).wait_recv()
            copy_d(m, p).start()

    def step_e(m):
        for p in range(2):
            copy_d(m, p).wait_recv()

    for group in range(groups):
        rate = jnp.broadcast_to(rates[group:group + 1, :], (128, group_rows)).T
        place = lax.broadcasted_iota(jnp.int32, (group_rows, 128), 0)
        scaling[group * group_rows:(group + 1) * group_rows, :] = jnp.where(place < counts[group, 0], rate, 0.0)

    input_copy(0).wait()
    input_copy(1).wait()

    @pl.loop(0, rows // tile)
    def _(index):
        at = pl.ds(pl.multiple_of(index * tile, tile), tile)
        tile_copy(index, 0).wait()
        k = keys[at, :]
        first_pre = dot(k, first[...])
        third_pre = dot(k, third[...])
        sig = jax.nn.sigmoid(first_pre)
        swish = first_pre * sig
        hidden_s[at, :] = (swish * third_pre).astype(BF16)
        swish_s[at, :] = swish
        gate_s[at, :] = third_pre * sig * (1.0 + first_pre * (1.0 - sig))
        tile_copy(index, 1).wait()
        scale = jnp.concatenate([scaling[at, :]] * (width // 128), axis=1)
        weighted_s[at, :] = (values[at, :].astype(F32) * scale).astype(BF16)

    wide[...] = dot(hidden_s[...], weighted_s[...], ((0,), (0,)))
    start_a(0)
    input_copy(2).wait()

    @pl.loop(0, rows // tile)
    def _(index):
        at = pl.ds(pl.multiple_of(index * tile, tile), tile)
        back = dot(weighted_s[at, :], second[...], ((1,), (1,)))
        back_third_s[at, :] = (back * swish_s[at, :]).astype(BF16)
        back_first_s[at, :] = (back * gate_s[at, :]).astype(BF16)

    step_b(0)
    wide[...] = dot(keys[...], back_third_s[...], ((0,), (0,)))
    start_a(1)
    wide[...] = dot(keys[...], back_first_s[...], ((0,), (0,)))
    start_a(2)
    step_c(0)
    step_b(1)
    step_d(0)
    step_e(0)

    def renew(weight, slot):
        old = weight[...].astype(F32)
        fresh = old + step_size * current[...].astype(F32)
        ratio = jnp.sqrt(jnp.mean(old * old, axis=0, keepdims=True) + 1e-06) / jnp.sqrt(
            jnp.mean(fresh * fresh, axis=0, keepdims=True) + 1e-06
        )
        fresh_w[slot] = (fresh * ratio).astype(BF16)

    @pl.loop(0, 3 * NS_ITERS)
    def _(t):
        @pl.when(t == NS_ITERS)
        def _():
            step_e(1)

        @pl.when(t == 2 * NS_ITERS)
        def _():
            step_e(2)

        @pl.when(t == 2 * NS_ITERS + 1)
        def _():
            for k in range(1, heads):
                weight_copy(k).wait_recv()
                weight_share(k).start()

        @pl.when(lax.rem(t, NS_ITERS) == 0)
        def _():
            m = t // NS_ITERS
            for index in range(shards):
                wide[index * grad_rows:(index + 1) * grad_rows, :] = full[m, index % 2, index // 2].astype(F32)
            gradient = wide[...]
            square = jnp.sum(jnp.sum(gradient * gradient, axis=0, keepdims=True), axis=1, keepdims=True)
            current[...] = (gradient / (jnp.sqrt(square) + 1e-06)).astype(BF16)

        gram_wide = dot(current[...], current[...], ((1,), (1,)))
        wide[...] = gram_wide
        gram_s[...] = gram_wide.astype(BF16)
        poly_s[...] = (coef_b * wide[...] + coef_c * dot(gram_s[...], gram_s[...])).astype(BF16)

        @pl.when(t == 0)
        def _():
            step_c(1)
            step_b(2)

        @pl.when(t == NS_ITERS - 1)
        def _():
            step_d(1)

        @pl.when(t == NS_ITERS)
        def _():
            step_c(2)

        @pl.when(t == 2 * NS_ITERS - 1)
        def _():
            step_d(2)

        current[...] = (coef_a * current[...].astype(F32) + dot(poly_s[...], current[...])).astype(BF16)

        @pl.when(t == NS_ITERS - 1)
        def _():
            renew(second, 2)

        @pl.when(t == 2 * NS_ITERS - 1)
        def _():
            renew(third, 1)

        @pl.when(t == 3 * NS_ITERS - 1)
        def _():
            renew(first, 0)

    gather_half = head_out.at[pl.ds(0, part)]
    last = heads - 1
    sides = {
        "right": (z, z + 1, ag_right, rs_right, rs_send_right, 0),
        "left": (last - z, z - 1, ag_left, rs_left, rs_send_left, 1),
    }

    def ag_copy(side, k):
        place, neighbour, slots, _, _, d = sides[side]
        source = gather_half if k == 1 else slots.at[k - 2]
        return remote(source, slots.at[k - 1], (sem_ag.at[0, d, k], sem_ag.at[1, d, k]), {"head": neighbour})

    def rs_copy(side, k):
        place, neighbour, _, slots, sends, d = sides[side]
        return remote(sends.at[k - 1], slots.at[k - 1], (sem_rs.at[0, d, k], sem_rs.at[1, d, k]), {"head": neighbour})

    def projected(dest):
        cols = pl.ds(pl.multiple_of(dest * width, 128), width)
        return dot(head_out[part:, :], out_weight[:, cols])

    def sums_out(side, k):
        place, _, _, slots, sends, _ = sides[side]

        @pl.when((place <= k - 1) & (place < last))
        def _():
            dest = heads - k + z if side == "right" else k + z - heads
            mine = projected(dest)
            if k == 1:
                sends[0] = mine.astype(BF16)
            else:
                @pl.when(place == 0)
                def _():
                    sends[k - 1] = mine.astype(BF16)

                @pl.when(place >= 1)
                def _():
                    rs_copy(side, k - 1).wait_recv()
                    sends[k - 1] = (mine + slots[k - 2].astype(F32)).astype(BF16)

            rs_copy(side, k).start()

    def gather_out(side, k):
        place = sides[side][0]

        @pl.when(place >= k - 1)
        def _():
            if k > 1:
                ag_copy(side, k - 1).wait_recv()

            @pl.when(place < last)
            def _():
                ag_copy(side, k).start()

    def round_sends(side, k):
        sums_out(side, k)
        gather_out(side, k)

    def gathered(side, k):
        place, _, slots, _, _, _ = sides[side]

        @pl.when(place >= k)
        def _():
            origin = z - k if side == "right" else z + k
            total_ag[...] += dot(slots[k - 1], columns[origin])

    input_copy(3).wait()
    input_copy(4).wait()
    at_end = jnp.where((z == 0) | (z == last), 1, 0)

    @pl.loop(0, 2)
    def _(turn):
        index = lax.rem(turn + at_end, 2)
        at = pl.ds(pl.multiple_of(index * part, part), part)
        q = queries[at, :]
        first_pre = dot(q, fresh_w[0])
        third_pre = dot(q, fresh_w[1])
        hidden = (first_pre * jax.nn.sigmoid(first_pre) * third_pre).astype(BF16)
        place = lax.broadcasted_iota(jnp.int32, (part, width), 0) + index * part
        head_out[at, :] = jnp.where(place < counts[groups, 0], dot(hidden, fresh_w[2]), 0.0).astype(BF16)

        @pl.when(index == 1)
        def _():
            sums_out("left", 1)
            sums_out("right", 1)

        @pl.when(index == 0)
        def _():
            gather_out("left", 1)
            gather_out("right", 1)

    own = pl.ds(pl.multiple_of(z * width, 128), width)
    total_ag[...] = dot(head_out[:part, :], out_weight[:, own])
    wide[:part, :] = projected(z)
    for j in range(1, heads):
        weight_share(j).wait_recv()

    for k in range(2, heads):
        @pl.when(2 * z < heads)
        def _():
            round_sends("left", k)
            round_sends("right", k)

        @pl.when(2 * z >= heads)
        def _():
            round_sends("right", k)
            round_sends("left", k)

        gathered("left", k - 1)
        gathered("right", k - 1)

    for side in ("left", "right"):
        place, _, ag_slots, rs_slots, _, _ = sides[side]

        @pl.when(place >= last)
        def _():
            ag_copy(side, last).wait_recv()

        gathered(side, last)

        @pl.when(place >= 1)
        def _():
            rs_copy(side, last).wait_recv()
            wide[:part, :] += rs_slots[last - 1].astype(F32)

    mixed[:part, :] = total_ag[...].astype(BF16)
    mixed[part:, :] = wide[:part, :].astype(BF16)

    for m in range(3):
        copy_a(m).wait_send()
        for p in range(2):
            copy_d(m, p).wait_send()
            for k in range(1, chips):
                copy_b(m, k, p).wait_send()
                copy_c(m, k, p).wait_send()
    for k in range(1, heads):
        weight_copy(k).wait_send()
        weight_share(k).wait_send()
        for side in ("left", "right"):
            place = sides[side][0]

            @pl.when((place <= k - 1) & (place < last))
            def _():
                rs_copy(side, k).wait_send()

            @pl.when((place >= k - 1) & (place < last))
            def _():
                ag_copy(side, k).wait_send()


def on_device(
    heads, shards,
    keys, values, step_rates, queries, first_weight, third_weight, second_weight, out_weight, live_counts,
):
    groups, rows, width = keys.shape
    chips = shards // 2
    grad_rows = width // shards
    part = rows // 2
    every = groups * rows
    tile = 256
    vmem = pl.BlockSpec(memory_space=pltpu.VMEM)
    hbm = pl.BlockSpec(memory_space=pl.ANY)
    dma = pltpu.SemaphoreType.DMA
    return pl.pallas_call(
        functools.partial(kernel, heads, shards, tile),
        out_shape=jax.ShapeDtypeStruct((rows, width), BF16),
        in_specs=[hbm, hbm, vmem, hbm, hbm, hbm, hbm, hbm, pl.BlockSpec(memory_space=pltpu.SMEM)],
        out_specs=vmem,
        scratch_shapes=[
            pltpu.VMEM((every, width), BF16),
            pltpu.VMEM((every, width), BF16),
            pltpu.VMEM((rows, width), BF16),
            pltpu.VMEM((width, width), BF16),
            pltpu.VMEM((width, width), BF16),
            pltpu.VMEM((width, width), BF16),
            pltpu.VMEM(out_weight.shape, BF16),
            pltpu.VMEM((every, 128), F32),
            pltpu.VMEM((every, width), F32),
            pltpu.VMEM((every, width), F32),
            pltpu.VMEM((every, width), BF16),
            pltpu.VMEM((every, width), BF16),
            pltpu.VMEM((every, width), BF16),
            pltpu.VMEM((every, width), BF16),
            pltpu.VMEM((width, width), F32),
            pltpu.VMEM((width, width), BF16),
            pltpu.VMEM((width, width), BF16),
            pltpu.VMEM((width, width), BF16),
            pltpu.VMEM((3, width, width), BF16),
            pltpu.VMEM((3, 2, chips, grad_rows, width), BF16),
            pltpu.VMEM((3, chips, grad_rows, width), BF16),
            pltpu.VMEM((3, chips, grad_rows, width), BF16),
            pltpu.VMEM((3, chips - 1, grad_rows, width), BF16),
            pltpu.VMEM((3, 2, chips, grad_rows, width), BF16),
            pltpu.VMEM((heads, width, width), BF16),
            pltpu.VMEM((rows, width), BF16),
        ]
        + [pltpu.VMEM((heads - 1, part, width), BF16)] * 6
        + [
            pltpu.VMEM((part, width), F32),
            dma((2, 3)),
            dma((2, 3, chips, 2)),
            dma((2, 3, chips, 2)),
            dma((2, 3, 2)),
            dma((2, heads)),
            dma((2, heads)),
            dma((2, 2, heads)),
            dma((2, 2, heads)),
            dma((5,)),
            dma((2, every // tile)),
        ],
        compiler_params=pltpu.CompilerParams(
            collective_id=0, has_side_effects=True, vmem_limit_bytes=67000000
        ),
        name="fast_weight_layer",
    )(
        keys.reshape(every, width), values.reshape(every, width), step_rates[:, 0], queries,
        first_weight[0], third_weight[0], second_weight[0], out_weight, live_counts,
    )


def solution(mesh):
    in_specs = (
        P(None, "seq", "head"),
        P(None, "seq", "head"),
        P(None, "head", "seq"),
        P("seq", "head"),
        P("head", None, None),
        P("head", None, None),
        P("head", None, None),
        P("head", None),
        P(None, "seq"),
    )
    return jax.shard_map(
        functools.partial(on_device, mesh.shape["head"], mesh.shape["seq"]),
        mesh=mesh, in_specs=in_specs, out_specs=P("seq", "head"), check_vma=False,
    )
```
